32 devices in a mesh: section: 2 (over x), tile: 16 (over z, y, core).
Axes of the slice: x: 2, y: 2, z: 4, core: 2. Of those that a mesh axis runs over, the one named last changes fastest.
Arguments:
- features: bfloat16 [16, 12, 1024, 128], P('tile', 'section'), may hold values from -6 to 6
- conv_weight: bfloat16 [5, 5, 128, 128], replicated, may hold values from -0.109375 to 0.109375
- head_weight: bfloat16 [128, 16], replicated, may hold values from -0.5 to 0.5
- kernels: bfloat16 [128, 1024, 2048], P('tile'), may hold values from -0.015625 to 0.015625
- source_weights: float32 [8], replicated, may hold values from 0.3 to 3
Outputs:
- intensity: float32 [16, 12, 1024], P('tile', 'section')
The draws below stay inside these ranges and needn't reach their ends.
All inputs are finite; a program needn't handle non-finite values.
Results may differ from the reference program's by a relative error of at most 0.0018.
Values may be sent and summed in bfloat16 or wider, within the bound.
A program may use at most 128 MiB of HBM per device.

```python
import math
import jax
import jax.numpy as jnp
from jax import lax

C = 128
K = 16
ANG = 8
W = 1024
TILES = 16
ROWS = 12


def steps_of(stream_key, shape, split, least, largest):
    gain = 1.0
    for axis_at, shards_of in split:
        draws = jax.random.uniform(jax.random.fold_in(jax.random.fold_in(stream_key, 6), axis_at), (shards_of,), jnp.float32, least / len(split), largest / len(split))
        gain = gain * jnp.repeat(jnp.exp(draws), shape[axis_at] // shards_of).reshape((-1,) + (1,) * (len(shape) - 1 - axis_at))
    return gain


def centred(rng, extent, scale, bound, shards=(), held_as=jnp.bfloat16):
    values = scale * jax.random.normal(rng, extent, jnp.float32)
    if shards:
        values = values * steps_of(rng, extent, shards, -0.22, 0.18)
    return jnp.clip(values, -bound, bound).astype(held_as)


def setup_inputs(seed: int = 0) -> dict:
    keys = jax.random.split(jax.random.key(seed), 6)
    return {
        "features": centred(keys[0], (TILES, ROWS, W, C), 1.0, 6.0, ((0, 16), (1, 2))),
        "conv_weight": centred(keys[1], (5, 5, C, C), (25 * C) ** -0.5, 0.109375),
        "head_weight": centred(keys[2], (C, 2 * ANG), C ** -0.5, 0.5),
        "kernels": centred(keys[3], (ANG * K, W, 2 * W), (W * K * ANG) ** -0.5, 0.015625, ((0, 16),)),
        "source_weights": jnp.clip(jnp.exp(jax.random.uniform(keys[4], (ANG,), jnp.float32, math.log(0.3), math.log(3.0))), 0.3, 3.0),
    }


def socs_image(field, operators):
    pixels = field.shape[-1]
    product = jnp.einsum('prw,kwv->pkrv', field.astype(jnp.float32), operators.astype(jnp.float32))
    real_part = product[0, :, :, :pixels] - product[1, :, :, pixels:]
    imag_part = product[0, :, :, pixels:] + product[1, :, :, :pixels]
    return jnp.sum(real_part * real_part + imag_part * imag_part, axis=0)


def reference(features, conv_weight, head_weight, kernels, source_weights):
    operators = kernels.reshape(ANG, K, kernels.shape[1], kernels.shape[2])

    def one_tile(window):
        preact = lax.conv_general_dilated(window[None], conv_weight, (1, 1), ((4, 4), (4, 4)), rhs_dilation=(2, 2), dimension_numbers=('NHWC', 'HWIO', 'NHWC'), preferred_element_type=jnp.float32)[0]
        hidden = jax.nn.gelu(preact, approximate=True).astype(jnp.bfloat16)
        near_field = jnp.einsum('rwc,cd->drw', hidden.astype(jnp.float32), head_weight.astype(jnp.float32)).astype(jnp.bfloat16)
        near_field = near_field.reshape(ANG, 2, near_field.shape[1], near_field.shape[2])
        running = jnp.zeros(near_field.shape[2:], jnp.float32)
        for angle_id in range(ANG):
            running = running + source_weights[angle_id] * socs_image(near_field[angle_id], operators[angle_id])
        return running
    return lax.map(one_tile, features)
```

```python
import functools

import jax
import jax.numpy as jnp
from jax import lax
from jax.experimental import pallas as pl
from jax.experimental.pallas import tpu as pltpu
from jax.sharding import PartitionSpec as P

ANG = 8
TAPS = 5
BIG = 256
SMALL = 128
SMALLS = 2
PAD = 16
SLOT = 16
SENDS = 2
MESH = pl.DeviceIdType.MESH


def kernel(tiles, groups, feat, conv_w, head_t, operators, source_w, out_ref,
           x_ref, w_ref, l_ref, h_ref, hb_ref, p_ref, ns_ref, nr_ref, e_ref, acc_ref, g_ref,
           s_ref, cx_ref, r_ref, rr_ref,
           own_sem, w_sem, g_sem, halo_send, halo_recv, near_send, near_recv,
           cx_send, cx_recv, ret_send, ret_recv):
    bf16, f32 = jnp.bfloat16, jnp.float32
    sec = lax.axis_index("section")
    me = lax.axis_index("tile")
    side = lax.rem(me, 2)
    sibling = me + 1 - 2 * side
    half, pixels, chans = feat.shape[0], feat.shape[2], feat.shape[3]
    units = 2 * half
    pairs = units // 2
    kers = operators.shape[0]
    bigs = (pixels - SMALLS * SMALL) // BIG
    edges = [c * BIG for c in range(bigs)] + [bigs * BIG + s * SMALL for s in range(SMALLS)] + [pixels]
    chunks = len(edges) - 1
    span = TAPS * 2 * chans
    wide = 2 * chans
    rows = tiles * units
    side_rows = rows // 2
    bt = min(tiles, 16)
    block_rows = bt * units
    vw = 256
    part_v = pixels // vw
    per_send = part_v // SENDS
    pw = pixels // SENDS
    unroll = min(kers, 8)

    own = pltpu.make_async_copy(
        feat.at[:, sec], x_ref.at[pl.ds(sec * half, half), pl.ds(PAD, pixels), :], own_sem)
    own.start()
    w_copies = []
    for d in range(3):
        for si in range(2):
            for so in range(2):
                tap = 2 * d + si - so
                if 0 <= tap < TAPS:
                    copy = pltpu.make_async_copy(
                        conv_w.at[tap],
                        w_ref.at[d, :, pl.ds(si * chans, chans), pl.ds(so * chans, chans)],
                        w_sem.at[len(w_copies)])
                    copy.start()
                    w_copies.append(copy)

    barrier = pltpu.get_barrier_semaphore()

    def greet(i, carry):
        pl.semaphore_signal(
            barrier, inc=1, device_id=(sec, lax.rem(me + i, tiles)), device_id_type=MESH)
        return carry

    def greet_across(i, carry):
        pl.semaphore_signal(
            barrier, inc=1, device_id=(1 - sec, lax.rem(me + 2 * i, tiles)), device_id_type=MESH)
        return carry

    lax.fori_loop(0, tiles // 2, greet_across, 0)
    lax.fori_loop(1, tiles, greet, 0)
    pl.semaphore_wait(barrier, tiles - 1 + tiles // 2)

    halos = []
    for c in range(chunks):
        lo = 0 if c == 0 else edges[c] + PAD
        hi = pixels if c == chunks - 1 else edges[c + 1] + PAD
        copy = pltpu.make_async_remote_copy(
            src_ref=feat.at[:, 1 - sec, pl.ds(lo, hi - lo), :],
            dst_ref=x_ref.at[pl.ds(sec * half, half), pl.ds(PAD + lo, hi - lo), :],
            send_sem=halo_send, recv_sem=halo_recv.at[c],
            device_id=(1 - sec, me), device_id_type=MESH)
        copy.start()
        halos.append(copy)

    g_copies = []
    for k in range(kers):
        copy = pltpu.make_async_copy(operators.at[k], g_ref.at[k], g_sem.at[k])
        copy.start()
        g_copies.append(copy)

    for d in range(3):
        for si in range(2):
            for so in range(2):
                if not 0 <= 2 * d + si - so < TAPS:
                    w_ref[d, :, si * chans:(si + 1) * chans, so * chans:(so + 1) * chans] = jnp.zeros(
                        (TAPS, chans, chans), bf16)
    edge = jnp.zeros((units, PAD, chans), bf16)
    x_ref[:, 0:PAD, :] = edge
    x_ref[:, PAD + pixels:, :] = edge

    lanes = ANG * SLOT
    col = lax.broadcasted_iota(jnp.int32, (lanes, 2 * ANG), 0)
    chan = lax.broadcasted_iota(jnp.int32, (lanes, 2 * ANG), 1)
    at = SLOT * (chan // 2) + units * lax.rem(chan, 2)
    for u in range(units):
        pick = jnp.where(col == at + u, 1.0, 0.0).astype(bf16)
        spread = jnp.dot(pick, head_t[...], preferred_element_type=f32)
        hb_ref[u * chans:(u + 1) * chans, :] = spread.T.astype(bf16)

    line = lax.broadcasted_iota(jnp.int32, (2 * block_rows, bt * SLOT), 0)
    slot = lax.broadcasted_iota(jnp.int32, (2 * block_rows, bt * SLOT), 1)
    part = line // block_rows
    line = line - part * block_rows
    core = line // (block_rows // 2)
    line = line - core * (block_rows // 2)
    tile = line // units
    unit = line - tile * units
    p_ref[...] = jnp.where(
        slot == (2 * tile + core) * SLOT + part * units + unit, 1.0, 0.0).astype(bf16)

    acc_ref[...] = jnp.zeros_like(acc_ref)
    own.wait()
    for copy in w_copies:
        copy.wait()

    def near_go(c, lo, cw):
        def source(peer):
            return ns_ref.at[pl.ds(pl.multiple_of(SLOT * (peer // groups), SLOT), SLOT), pl.ds(lo, cw)]

        target = nr_ref.at[pl.ds(pl.multiple_of(SLOT * me, SLOT), SLOT), pl.ds(lo, cw)]

        def send(i, inner):
            peer = lax.rem(me + i, tiles)
            pltpu.make_async_remote_copy(
                src_ref=source(peer), dst_ref=target, send_sem=near_send.at[c],
                recv_sem=near_recv.at[c], device_id=(sec, peer), device_id_type=MESH).start()
            return inner

        lax.fori_loop(1, tiles, send, 0)
        pltpu.make_async_copy(source(me), target, near_recv.at[c]).start()

    def conv(c, lo, cw):
        def build(u):
            window = x_ref[u, pl.ds(lo, cw + 2 * PAD), :]
            for j in range(TAPS):
                first = PAD + 2 * j - (TAPS - 1)
                at = (u // 2) * span + j * wide + (u % 2) * chans
                l_ref[0:cw, at:at + chans] = window[first:first + cw, :]

        build(0)
        build(1)
        for p in range(pairs):
            if p + 1 < pairs:
                build(2 * p + 2)
                build(2 * p + 3)
            d0, d1 = max(p - 1, 0), min(p + 1, pairs - 1)
            w0, w1 = d0 - p + 1, d1 - p + 2
            pre = jnp.dot(
                l_ref[0:cw, d0 * span:(d1 + 1) * span],
                w_ref[w0:w1].reshape((w1 - w0) * span, wide),
                preferred_element_type=f32)
            h_ref[0:cw, p * wide:(p + 1) * wide] = jax.nn.gelu(pre, approximate=True).astype(bf16)
        near = jnp.dot(h_ref[0:cw, :], hb_ref[...], preferred_element_type=f32)
        ns_ref[:, pl.ds(lo, cw)] = near.T.astype(bf16)
        near_go(c, lo, cw)

    def gather(c, lo, cw):
        arrived = nr_ref.at[:, pl.ds(lo, cw)]
        pltpu.make_async_copy(arrived, arrived, near_recv.at[c]).wait()
        for b in range(tiles // bt):
            field = jnp.dot(
                p_ref[...], nr_ref[b * bt * SLOT:(b + 1) * bt * SLOT, pl.ds(lo, cw)],
                preferred_element_type=f32).astype(bf16)
            for core in range(2):
                n = block_rows // 2
                real = field[core * n:(core + 1) * n]
                imag = field[block_rows + core * n:block_rows + (core + 1) * n]
                at = core * side_rows + b * n
                e_ref[at:at + n, 0:cw] = real
                e_ref[rows + at:rows + at + n, 0:cw] = imag
                e_ref[at:at + n, cw:2 * cw] = -imag
                e_ref[rows + at:rows + at + n, cw:2 * cw] = real

    def product(lo, cw, v, k):
        at = v * vw
        if cw < BIG:
            both = jnp.concatenate(
                [g_ref[k, pl.ds(lo, cw), at:at + vw],
                 g_ref[k, pl.ds(lo, cw), pixels + at:pixels + at + vw]], axis=0)
            return jnp.dot(e_ref[:, 0:2 * cw], both, preferred_element_type=f32)
        amp = jnp.dot(e_ref[:, 0:cw], g_ref[k, pl.ds(lo, cw), at:at + vw],
                      preferred_element_type=f32)
        return amp + jnp.dot(e_ref[:, cw:2 * cw],
                             g_ref[k, pl.ds(lo, cw), pixels + at:pixels + at + vw],
                             preferred_element_type=f32)

    def images(lo, cw):
        def image(kb, inner):
            for i in range(unroll):
                for v in range(part_v):
                    acc_ref[kb * unroll + i, v] += product(lo, cw, v, kb * unroll + i)
            return inner

        lax.fori_loop(0, kers // unroll, image, 0)

    def step(c, carry):
        for cc in range(bigs):
            @pl.when(c == cc)
            def _():
                halos[cc].wait_recv()

        @pl.when(c < bigs)
        def _():
            conv(c, pl.multiple_of(c * BIG, BIG), BIG)

        @pl.when(c == bigs)
        def _():
            def small(s, inner):
                for ss in range(SMALLS):
                    @pl.when(s == ss)
                    def _():
                        halos[bigs + ss].wait_recv()
                conv(bigs + s, pl.multiple_of(bigs * BIG + s * SMALL, SMALL), SMALL)
                return inner

            lax.fori_loop(0, SMALLS, small, 0)

        @pl.when(c == 1)
        def _():
            for copy in g_copies:
                copy.wait()

        @pl.when(c > 0)
        def _():
            lo = pl.multiple_of((c - 1) * BIG, BIG)
            gather(c - 1, lo, BIG)
            images(lo, BIG)

        return carry

    lax.fori_loop(0, bigs + 1, step, 0)
    for c in range(bigs, chunks - 1):
        gather(c, edges[c], SMALL)
        images(edges[c], SMALL)
    gather(chunks - 1, edges[-2], SMALL)

    weight = source_w[me // groups]
    cx_copies = []
    for n in range(SENDS):
        for m in range(per_send):
            v = n * per_send + m

            def power(kb, total):
                for i in range(unroll):
                    k = kb * unroll + i
                    amp = acc_ref[k, v] + product(edges[-2], SMALL, v, k)
                    square = amp * amp
                    total = total + (square[0:rows] + square[rows:])
                return total

            total = jnp.zeros((rows, vw), f32)
            if kers == unroll:
                total = power(0, total)
            else:
                total = lax.fori_loop(0, kers // unroll, power, total)
            s_ref[:, v * vw:(v + 1) * vw] = total * weight
        copy = pltpu.make_async_remote_copy(
            src_ref=s_ref.at[pl.ds(pl.multiple_of((1 - side) * side_rows, 16), side_rows),
                             pl.ds(n * pw, pw)],
            dst_ref=cx_ref.at[n], send_sem=cx_send.at[n], recv_sem=cx_recv.at[n],
            device_id=(sec, sibling), device_id_type=MESH)
        copy.start()
        cx_copies.append(copy)

    chip = me // 2
    chips = tiles // 2

    def ret_copy(n, h, i):
        return pltpu.make_async_remote_copy(
            src_ref=r_ref.at[n, i, h], dst_ref=rr_ref.at[n, sec, chip],
            send_sem=ret_send.at[n], recv_sem=ret_recv.at[n],
            device_id=(h, 2 * i + side), device_id_type=MESH)

    for n in range(SENDS):
        cx_copies[n].wait_recv()
        mine = s_ref[pl.ds(pl.multiple_of(side * side_rows, 16), side_rows), n * pw:(n + 1) * pw]
        mine = mine + cx_ref[n]
        for i in range(chips):
            for h in range(2):
                first = i * units + h * half
                r_ref[n, i, h] = mine[first:first + half].astype(bf16)

        def ret_go(i, carry):
            peer = lax.rem(chip + i, chips)
            ret_copy(n, sec, peer).start()
            ret_copy(n, 1 - sec, peer).start()
            return carry

        lax.fori_loop(1, chips, ret_go, 0)
        ret_copy(n, 1 - sec, chip).start()
        pltpu.make_async_copy(r_ref.at[n, chip, sec], rr_ref.at[n, sec, chip], ret_recv.at[n]).start()

    for n in range(SENDS):
        pltpu.make_async_copy(rr_ref.at[n], rr_ref.at[n], ret_recv.at[n]).wait()
        for par in range(2):
            total = rr_ref[n, par, 0].astype(f32)
            for i in range(1, chips):
                total = total + rr_ref[n, par, i].astype(f32)
            for j in range(half):
                out_ref[0, 2 * j + par:2 * j + par + 1, n * pw:(n + 1) * pw] = total[j:j + 1]

    sent = feat.at[:, sec]
    pltpu.make_async_copy(sent, sent, halo_send).wait()
    for c in range(chunks):
        sent = nr_ref.at[pl.ds(0, (tiles - 1) * SLOT), pl.ds(edges[c], edges[c + 1] - edges[c])]
        pltpu.make_async_copy(sent, sent, near_send.at[c]).wait()
    for n in range(SENDS):
        cx_copies[n].wait_send()

        def ret_sent(i, carry):
            ret_copy(n, sec, 0).wait_send()
            ret_copy(n, 1 - sec, 0).wait_send()
            return carry

        lax.fori_loop(1, chips, ret_sent, 0)
        ret_copy(n, 1 - sec, 0).wait_send()


def on_device(features, conv_weight, head_weight, kernels, source_weights):
    tiles = lax.axis_size("tile")
    groups = tiles // ANG
    _, rows_dev, pixels, chans = features.shape
    half = rows_dev // 2
    units = 2 * half
    kers = kernels.shape[0]
    rows = tiles * units
    bt = min(tiles, 16)
    chunks = (pixels - SMALLS * SMALL) // BIG + SMALLS
    bf16, f32 = jnp.bfloat16, jnp.float32
    feat = features.reshape(half, 2, pixels, chans)
    any_spec = pl.BlockSpec(memory_space=pl.ANY)
    image = pl.pallas_call(
        functools.partial(kernel, tiles, groups),
        out_shape=jax.ShapeDtypeStruct((1, rows_dev, pixels), f32),
        in_specs=[
            any_spec,
            any_spec,
            pl.BlockSpec(memory_space=pltpu.VMEM),
            any_spec,
            pl.BlockSpec(memory_space=pltpu.SMEM),
        ],
        out_specs=pl.BlockSpec(memory_space=pltpu.VMEM),
        scratch_shapes=[
            pltpu.VMEM((units, pixels + 2 * PAD, chans), bf16),
            pltpu.VMEM((3, TAPS, 2 * chans, 2 * chans), bf16),
            pltpu.VMEM((BIG, (units // 2) * TAPS * 2 * chans), bf16),
            pltpu.VMEM((BIG, units * chans), bf16),
            pltpu.VMEM((units * chans, ANG * SLOT), bf16),
            pltpu.VMEM((2 * bt * units, bt * SLOT), bf16),
            pltpu.VMEM((ANG * SLOT, pixels), bf16),
            pltpu.VMEM((tiles * SLOT, pixels), bf16),
            pltpu.VMEM((2 * rows, 2 * BIG), bf16),
            pltpu.VMEM((kers, pixels // 256, 2 * rows, 256), f32),
            pltpu.VMEM((kers, pixels, 2 * pixels), bf16),
            pltpu.VMEM((rows, pixels), f32),
            pltpu.VMEM((SENDS, rows // 2, pixels // SENDS), f32),
            pltpu.VMEM((SENDS, tiles // 2, 2, half, pixels // SENDS), bf16),
            pltpu.VMEM((SENDS, 2, tiles // 2, half, pixels // SENDS), bf16),
            pltpu.SemaphoreType.DMA,
            pltpu.SemaphoreType.DMA((10,)),
            pltpu.SemaphoreType.DMA((kers,)),
            pltpu.SemaphoreType.DMA,
            pltpu.SemaphoreType.DMA((chunks,)),
            pltpu.SemaphoreType.DMA((chunks,)),
            pltpu.SemaphoreType.DMA((chunks,)),
            pltpu.SemaphoreType.DMA((SENDS,)),
            pltpu.SemaphoreType.DMA((SENDS,)),
            pltpu.SemaphoreType.DMA((SENDS,)),
            pltpu.SemaphoreType.DMA((SENDS,)),
        ],
        compiler_params=pltpu.CompilerParams(
            collective_id=0, has_side_effects=True, vmem_limit_bytes=66_000_000),
    )(feat, conv_weight, head_weight.T, kernels, source_weights)
    return image


def solution(mesh):
    in_specs = (P("tile", "section", None, None), P(), P(), P("tile", None, None), P())
    out_specs = P("tile", "section", None)
    return jax.shard_map(
        on_device, mesh=mesh, in_specs=in_specs, out_specs=out_specs, check_vma=False
    )
```

```python
import functools

import jax
import jax.numpy as jnp
from jax import lax
from jax.experimental import pallas as pl
from jax.experimental.pallas import tpu as pltpu
from jax.sharding import PartitionSpec as P

ANG = 8
TAPS = 5
BIG = 256
SMALL = 128
SMALLS = 2
PAD = 16
SLOT = 16
SENDS = 1
MESH = pl.DeviceIdType.MESH


def kernel(tiles, groups, feat, conv_w, head_t, operators, source_w, out_ref,
           x_ref, w_ref, l_ref, h_ref, hb_ref, p_ref, ns_ref, nr_ref, e_ref, acc_ref, g_ref,
           s_ref, cx_ref, r_ref, rr_ref,
           own_sem, w_sem, g_sem, halo_send, halo_recv, near_send, near_recv,
           cx_send, cx_recv, ret_send, ret_recv, met_sem, all_sem):
    bf16, f32 = jnp.bfloat16, jnp.float32
    sec = lax.axis_index("section")
    me = lax.axis_index("tile")
    side = lax.rem(me, 2)
    sibling = me + 1 - 2 * side
    half, pixels, chans = feat.shape[0], feat.shape[2], feat.shape[3]
    units = 2 * half
    pairs = units // 2
    kers = operators.shape[0]
    bigs = (pixels - SMALLS * SMALL) // BIG
    edges = [c * BIG for c in range(bigs)] + [bigs * BIG + s * SMALL for s in range(SMALLS)] + [pixels]
    chunks = len(edges) - 1
    span = TAPS * 2 * chans
    wide = 2 * chans
    rows = tiles * units
    side_rows = rows // 2
    bt = min(tiles, 16)
    block_rows = bt * units
    vw = 256
    part_v = pixels // vw
    per_send = part_v // SENDS
    pw = pixels // SENDS
    unroll = min(kers, 8)

    own = pltpu.make_async_copy(
        feat.at[:, sec], x_ref.at[pl.ds(sec * half, half), pl.ds(PAD, pixels), :], own_sem)
    own.start()
    w_copies = []
    for d in range(3):
        for si in range(2):
            for so in range(2):
                tap = 2 * d + si - so
                if 0 <= tap < TAPS:
                    copy = pltpu.make_async_copy(
                        conv_w.at[tap],
                        w_ref.at[d, :, pl.ds(si * chans, chans), pl.ds(so * chans, chans)],
                        w_sem.at[len(w_copies)])
                    copy.start()
                    w_copies.append(copy)

    barrier = pltpu.get_barrier_semaphore()

    @pl.when(sec == 1)
    def _():
        pl.semaphore_signal(barrier, inc=1, device_id=(0, me), device_id_type=MESH)

    @pl.when(sec == 0)
    def _():
        pl.semaphore_wait(barrier, 1)
        pl.semaphore_signal(met_sem, inc=1, device_id=(1, me), device_id_type=MESH)

    @pl.when(sec == 1)
    def _():
        pl.semaphore_wait(met_sem, 1)

    halos = []
    for c in range(chunks):
        lo = 0 if c == 0 else edges[c] + PAD
        hi = pixels if c == chunks - 1 else edges[c + 1] + PAD
        copy = pltpu.make_async_remote_copy(
            src_ref=feat.at[:, 1 - sec, pl.ds(lo, hi - lo), :],
            dst_ref=x_ref.at[pl.ds(sec * half, half), pl.ds(PAD + lo, hi - lo), :],
            send_sem=halo_send, recv_sem=halo_recv.at[c],
            device_id=(1 - sec, me), device_id_type=MESH)
        copy.start()
        halos.append(copy)

    @pl.when(sec == 1)
    def _():
        def greet(i, carry):
            pl.semaphore_signal(
                barrier, inc=1, device_id=(1, lax.rem(me + i, tiles)), device_id_type=MESH)
            return carry

        lax.fori_loop(1, tiles, greet, 0)

    g_copies = []
    for k in range(kers):
        copy = pltpu.make_async_copy(operators.at[k], g_ref.at[k], g_sem.at[k])
        copy.start()
        g_copies.append(copy)

    for d in range(3):
        for si in range(2):
            for so in range(2):
                if not 0 <= 2 * d + si - so < TAPS:
                    w_ref[d, :, si * chans:(si + 1) * chans, so * chans:(so + 1) * chans] = jnp.zeros(
                        (TAPS, chans, chans), bf16)
    edge = jnp.zeros((units, PAD, chans), bf16)
    x_ref[:, 0:PAD, :] = edge
    x_ref[:, PAD + pixels:, :] = edge

    lanes = ANG * SLOT
    col = lax.broadcasted_iota(jnp.int32, (lanes, 2 * ANG), 0)
    chan = lax.broadcasted_iota(jnp.int32, (lanes, 2 * ANG), 1)
    at = SLOT * (chan // 2) + units * lax.rem(chan, 2)
    for u in range(units):
        pick = jnp.where(col == at + u, 1.0, 0.0).astype(bf16)
        spread = jnp.dot(pick, head_t[...], preferred_element_type=f32)
        hb_ref[u * chans:(u + 1) * chans, :] = spread.T.astype(bf16)

    line = lax.broadcasted_iota(jnp.int32, (2 * block_rows, bt * SLOT), 0)
    slot = lax.broadcasted_iota(jnp.int32, (2 * block_rows, bt * SLOT), 1)
    part = line // block_rows
    line = line - part * block_rows
    core = line // (block_rows // 2)
    line = line - core * (block_rows // 2)
    tile = line // units
    unit = line - tile * units
    p_ref[...] = jnp.where(
        slot == (2 * tile + core) * SLOT + part * units + unit, 1.0, 0.0).astype(bf16)

    acc_ref[...] = jnp.zeros_like(acc_ref)
    own.wait()
    for copy in w_copies:
        copy.wait()

    @pl.when(sec == 1)
    def _():
        pl.semaphore_wait(barrier, tiles - 1)
        pl.semaphore_signal(all_sem, inc=1, device_id=(0, me), device_id_type=MESH)

    @pl.when(sec == 0)
    def _():
        pl.semaphore_wait(all_sem, 1)

    def near_go(c, lo, cw):
        def source(peer):
            return ns_ref.at[pl.ds(pl.multiple_of(SLOT * (peer // groups), SLOT), SLOT), pl.ds(lo, cw)]

        target = nr_ref.at[pl.ds(pl.multiple_of(SLOT * me, SLOT), SLOT), pl.ds(lo, cw)]

        def send(i, inner):
            peer = lax.rem(me + i, tiles)
            pltpu.make_async_remote_copy(
                src_ref=source(peer), dst_ref=target, send_sem=near_send.at[c],
                recv_sem=near_recv.at[c], device_id=(sec, peer), device_id_type=MESH).start()
            return inner

        lax.fori_loop(1, tiles, send, 0)
        pltpu.make_async_copy(source(me), target, near_recv.at[c]).start()

    def conv(c, lo, cw):
        def build(u):
            window = x_ref[u, pl.ds(lo, cw + 2 * PAD), :]
            for j in range(TAPS):
                first = PAD + 2 * j - (TAPS - 1)
                at = (u // 2) * span + j * wide + (u % 2) * chans
                l_ref[0:cw, at:at + chans] = window[first:first + cw, :]

        build(0)
        build(1)
        for p in range(pairs):
            if p + 1 < pairs:
                build(2 * p + 2)
                build(2 * p + 3)
            d0, d1 = max(p - 1, 0), min(p + 1, pairs - 1)
            w0, w1 = d0 - p + 1, d1 - p + 2
            pre = jnp.dot(
                l_ref[0:cw, d0 * span:(d1 + 1) * span],
                w_ref[w0:w1].reshape((w1 - w0) * span, wide),
                preferred_element_type=f32)
            h_ref[0:cw, p * wide:(p + 1) * wide] = jax.nn.gelu(pre, approximate=True).astype(bf16)
        near = jnp.dot(h_ref[0:cw, :], hb_ref[...], preferred_element_type=f32)
        ns_ref[:, pl.ds(lo, cw)] = near.T.astype(bf16)
        near_go(c, lo, cw)

    def gather(c, lo, cw):
        arrived = nr_ref.at[:, pl.ds(lo, cw)]
        pltpu.make_async_copy(arrived, arrived, near_recv.at[c]).wait()
        for b in range(tiles // bt):
            field = jnp.dot(
                p_ref[...], nr_ref[b * bt * SLOT:(b + 1) * bt * SLOT, pl.ds(lo, cw)],
                preferred_element_type=f32).astype(bf16)
            for core in range(2):
                n = block_rows // 2
                real = field[core * n:(core + 1) * n]
                imag = field[block_rows + core * n:block_rows + (core + 1) * n]
                at = core * side_rows + b * n
                e_ref[at:at + n, 0:cw] = real
                e_ref[rows + at:rows + at + n, 0:cw] = imag
                e_ref[at:at + n, cw:2 * cw] = -imag
                e_ref[rows + at:rows + at + n, cw:2 * cw] = real

    def product(lo, cw, v, k):
        at = v * vw
        if cw < BIG:
            both = jnp.concatenate(
                [g_ref[k, pl.ds(lo, cw), at:at + vw],
                 g_ref[k, pl.ds(lo, cw), pixels + at:pixels + at + vw]], axis=0)
            return jnp.dot(e_ref[:, 0:2 * cw], both, preferred_element_type=f32)
        amp = jnp.dot(e_ref[:, 0:cw], g_ref[k, pl.ds(lo, cw), at:at + vw],
                      preferred_element_type=f32)
        return amp + jnp.dot(e_ref[:, cw:2 * cw],
                             g_ref[k, pl.ds(lo, cw), pixels + at:pixels + at + vw],
                             preferred_element_type=f32)

    def images(lo, cw):
        def image(kb, inner):
            for i in range(unroll):
                for v in range(part_v):
                    acc_ref[kb * unroll + i, v] += product(lo, cw, v, kb * unroll + i)
            return inner

        lax.fori_loop(0, kers // unroll, image, 0)

    def step(c, carry):
        for cc in range(bigs):
            @pl.when(c == cc)
            def _():
                halos[cc].wait_recv()

        @pl.when(c < bigs)
        def _():
            conv(c, pl.multiple_of(c * BIG, BIG), BIG)

        @pl.when(c == bigs)
        def _():
            def small(s, inner):
                for ss in range(SMALLS):
                    @pl.when(s == ss)
                    def _():
                        halos[bigs + ss].wait_recv()
                conv(bigs + s, pl.multiple_of(bigs * BIG + s * SMALL, SMALL), SMALL)
                return inner

            lax.fori_loop(0, SMALLS, small, 0)

        @pl.when(c == 1)
        def _():
            for copy in g_copies:
                copy.wait()

        @pl.when(c > 0)
        def _():
            lo = pl.multiple_of((c - 1) * BIG, BIG)
            gather(c - 1, lo, BIG)
            images(lo, BIG)

        return carry

    lax.fori_loop(0, bigs + 1, step, 0)
    for c in range(bigs, chunks - 1):
        gather(c, edges[c], SMALL)
        images(edges[c], SMALL)
    gather(chunks - 1, edges[-2], SMALL)

    weight = source_w[me // groups]
    chip = me // 2
    chips = tiles // 2

    def ret_copy(n, h, i):
        return pltpu.make_async_remote_copy(
            src_ref=r_ref.at[n, i, h], dst_ref=rr_ref.at[n, sec, chip],
            send_sem=ret_send.at[n], recv_sem=ret_recv.at[n],
            device_id=(h, 2 * i + side), device_id_type=MESH)

    cx_copies = []

    def ret_block(n):
        cx_copies[n].wait_recv()
        mine = s_ref[pl.ds(pl.multiple_of(side * side_rows, 16), side_rows), n * pw:(n + 1) * pw]
        mine = mine + cx_ref[n]
        for i in range(chips):
            for h in range(2):
                first = i * units + h * half
                r_ref[n, i, h] = mine[first:first + half].astype(bf16)

        def ret_go(i, carry):
            peer = lax.rem(chip + i, chips)
            ret_copy(n, sec, peer).start()
            ret_copy(n, 1 - sec, peer).start()
            return carry

        lax.fori_loop(1, chips, ret_go, 0)
        ret_copy(n, 1 - sec, chip).start()
        pltpu.make_async_copy(r_ref.at[n, chip, sec], rr_ref.at[n, sec, chip], ret_recv.at[n]).start()

    for n in range(SENDS):
        for m in range(per_send):
            v = n * per_send + m

            def power(kb, total):
                for i in range(unroll):
                    k = kb * unroll + i
                    amp = acc_ref[k, v] + product(edges[-2], SMALL, v, k)
                    square = amp * amp
                    total = total + (square[0:rows] + square[rows:])
                return total

            total = jnp.zeros((rows, vw), f32)
            if kers == unroll:
                total = power(0, total)
            else:
                total = lax.fori_loop(0, kers // unroll, power, total)
            s_ref[:, v * vw:(v + 1) * vw] = total * weight
        copy = pltpu.make_async_remote_copy(
            src_ref=s_ref.at[pl.ds(pl.multiple_of((1 - side) * side_rows, 16), side_rows),
                             pl.ds(n * pw, pw)],
            dst_ref=cx_ref.at[n], send_sem=cx_send.at[n], recv_sem=cx_recv.at[n],
            device_id=(sec, sibling), device_id_type=MESH)
        copy.start()
        cx_copies.append(copy)
        if n:
            ret_block(n - 1)
    ret_block(SENDS - 1)

    for n in range(SENDS):
        pltpu.make_async_copy(rr_ref.at[n], rr_ref.at[n], ret_recv.at[n]).wait()
        for par in range(2):
            total = rr_ref[n, par, 0].astype(f32)
            for i in range(1, chips):
                total = total + rr_ref[n, par, i].astype(f32)
            for j in range(half):
                out_ref[0, 2 * j + par:2 * j + par + 1, n * pw:(n + 1) * pw] = total[j:j + 1]

    sent = feat.at[:, sec]
    pltpu.make_async_copy(sent, sent, halo_send).wait()
    for c in range(chunks):
        sent = nr_ref.at[pl.ds(0, (tiles - 1) * SLOT), pl.ds(edges[c], edges[c + 1] - edges[c])]
        pltpu.make_async_copy(sent, sent, near_send.at[c]).wait()
    for n in range(SENDS):
        cx_copies[n].wait_send()

        def ret_sent(i, carry):
            ret_copy(n, sec, 0).wait_send()
            ret_copy(n, 1 - sec, 0).wait_send()
            return carry

        lax.fori_loop(1, chips, ret_sent, 0)
        ret_copy(n, 1 - sec, 0).wait_send()


def on_device(features, conv_weight, head_weight, kernels, source_weights):
    tiles = lax.axis_size("tile")
    groups = tiles // ANG
    _, rows_dev, pixels, chans = features.shape
    half = rows_dev // 2
    units = 2 * half
    kers = kernels.shape[0]
    rows = tiles * units
    bt = min(tiles, 16)
    chunks = (pixels - SMALLS * SMALL) // BIG + SMALLS
    bf16, f32 = jnp.bfloat16, jnp.float32
    feat = features.reshape(half, 2, pixels, chans)
    any_spec = pl.BlockSpec(memory_space=pl.ANY)
    image = pl.pallas_call(
        functools.partial(kernel, tiles, groups),
        out_shape=jax.ShapeDtypeStruct((1, rows_dev, pixels), f32),
        in_specs=[
            any_spec,
            any_spec,
            pl.BlockSpec(memory_space=pltpu.VMEM),
            any_spec,
            pl.BlockSpec(memory_space=pltpu.SMEM),
        ],
        out_specs=pl.BlockSpec(memory_space=pltpu.VMEM),
        scratch_shapes=[
            pltpu.VMEM((units, pixels + 2 * PAD, chans), bf16),
            pltpu.VMEM((3, TAPS, 2 * chans, 2 * chans), bf16),
            pltpu.VMEM((BIG, (units // 2) * TAPS * 2 * chans), bf16),
            pltpu.VMEM((BIG, units * chans), bf16),
            pltpu.VMEM((units * chans, ANG * SLOT), bf16),
            pltpu.VMEM((2 * bt * units, bt * SLOT), bf16),
            pltpu.VMEM((ANG * SLOT, pixels), bf16),
            pltpu.VMEM((tiles * SLOT, pixels), bf16),
            pltpu.VMEM((2 * rows, 2 * BIG), bf16),
            pltpu.VMEM((kers, pixels // 256, 2 * rows, 256), f32),
            pltpu.VMEM((kers, pixels, 2 * pixels), bf16),
            pltpu.VMEM((rows, pixels), f32),
            pltpu.VMEM((SENDS, rows // 2, pixels // SENDS), f32),
            pltpu.VMEM((SENDS, tiles // 2, 2, half, pixels // SENDS), bf16),
            pltpu.VMEM((SENDS, 2, tiles // 2, half, pixels // SENDS), bf16),
            pltpu.SemaphoreType.DMA,
            pltpu.SemaphoreType.DMA((10,)),
            pltpu.SemaphoreType.DMA((kers,)),
            pltpu.SemaphoreType.DMA,
            pltpu.SemaphoreType.DMA((chunks,)),
            pltpu.SemaphoreType.DMA((chunks,)),
            pltpu.SemaphoreType.DMA((chunks,)),
            pltpu.SemaphoreType.DMA((SENDS,)),
            pltpu.SemaphoreType.DMA((SENDS,)),
            pltpu.SemaphoreType.DMA((SENDS,)),
            pltpu.SemaphoreType.DMA((SENDS,)),
            pltpu.SemaphoreType.REGULAR,
            pltpu.SemaphoreType.REGULAR,
        ],
        compiler_params=pltpu.CompilerParams(
            collective_id=0, has_side_effects=True, vmem_limit_bytes=66_000_000),
    )(feat, conv_weight, head_weight.T, kernels, source_weights)
    return image


def solution(mesh):
    in_specs = (P("tile", "section", None, None), P(), P(), P("tile", None, None), P())
    out_specs = P("tile", "section", None)
    return jax.shard_map(
        on_device, mesh=mesh, in_specs=in_specs, out_specs=out_specs, check_vma=False
    )
```

```python
import functools

import jax
import jax.numpy as jnp
from jax import lax
from jax.experimental import pallas as pl
from jax.experimental.pallas import tpu as pltpu
from jax.sharding import PartitionSpec as P

ANG = 8
TAPS = 5
BIG = 256
SMALL = 128
SMALLS = 2
PAD = 16
SLOT = 16
SENDS = 1
MESH = pl.DeviceIdType.MESH


def kernel(tiles, groups, feat, conv_w, head_t, operators, source_w, out_ref,
           x_ref, w_ref, l_ref, a_ref, h_ref, hb_ref, p_ref, ns_ref, nr_ref, e_ref, acc_ref, g_ref,
           s_ref, cx_ref, r_ref, rr_ref,
           own_sem, w_sem, g_sem, halo_send, halo_recv, near_send, near_recv,
           cx_send, cx_recv, ret_send, ret_recv, met_sem, all_sem):
    bf16, f32 = jnp.bfloat16, jnp.float32
    sec = lax.axis_index("section")
    me = lax.axis_index("tile")
    side = lax.rem(me, 2)
    sibling = me + 1 - 2 * side
    half, pixels, chans = feat.shape[0], feat.shape[2], feat.shape[3]
    units = 2 * half
    pairs = units // 2
    kers = operators.shape[0]
    bigs = (pixels - SMALLS * SMALL) // BIG
    edges = [c * BIG for c in range(bigs)] + [bigs * BIG + s * SMALL for s in range(SMALLS)] + [pixels]
    chunks = len(edges) - 1
    span = TAPS * 2 * chans
    wide = 2 * chans
    rows = tiles * units
    side_rows = rows // 2
    bt = min(tiles, 16)
    block_rows = bt * units
    vw = 256
    part_v = pixels // vw
    per_send = part_v // SENDS
    pw = pixels // SENDS
    unroll = min(kers, 8)

    barrier = pltpu.get_barrier_semaphore()
    root = jnp.logical_and(me == 0, sec == 0)
    beside = jnp.logical_and(me == 0, sec == 1)

    @pl.when(jnp.logical_not(beside))
    def _():
        pl.semaphore_signal(barrier, inc=1, device_id=(1 - sec, me), device_id_type=MESH)

    def mirrored(i):
        return i + sec * (pairs - 1 - 2 * i)

    own = pltpu.make_async_copy(
        feat.at[:, sec], x_ref.at[pl.ds(sec * half, half), pl.ds(PAD, pixels), :], own_sem)
    own.start()
    w_copies = []
    for d in range(3):
        for si in range(2):
            for so in range(2):
                tap = 2 * d + si - so
                if 0 <= tap < TAPS:
                    copy = pltpu.make_async_copy(
                        conv_w.at[tap],
                        w_ref.at[mirrored(d), :, pl.ds(si * chans, chans), pl.ds(so * chans, chans)],
                        w_sem.at[len(w_copies)])
                    copy.start()
                    w_copies.append(copy)

    @pl.when(jnp.logical_not(root))
    def _():
        pl.semaphore_wait(barrier, 1)

    @pl.when(beside)
    def _():
        pl.semaphore_signal(met_sem, inc=1, device_id=(0, 0), device_id_type=MESH)

    @pl.when(root)
    def _():
        pl.semaphore_wait(met_sem, 1)

    halos = []
    for c in range(chunks):
        lo = 0 if c == 0 else edges[c] + PAD
        hi = pixels if c == chunks - 1 else edges[c + 1] + PAD
        copy = pltpu.make_async_remote_copy(
            src_ref=feat.at[:, 1 - sec, pl.ds(lo, hi - lo), :],
            dst_ref=x_ref.at[pl.ds(sec * half, half), pl.ds(PAD + lo, hi - lo), :],
            send_sem=halo_send, recv_sem=halo_recv.at[c],
            device_id=(1 - sec, me), device_id_type=MESH)
        copy.start()
        halos.append(copy)

    @pl.when(jnp.logical_and(me > 0, sec == 0))
    def _():
        pl.semaphore_signal(barrier, inc=1, device_id=(0, 0), device_id_type=MESH)

    g_copies = []
    for k in range(kers):
        copy = pltpu.make_async_copy(operators.at[k], g_ref.at[k], g_sem.at[k])
        copy.start()
        g_copies.append(copy)

    for d in range(3):
        for si in range(2):
            for so in range(2):
                if not 0 <= 2 * d + si - so < TAPS:
                    w_ref[mirrored(d), :, si * chans:(si + 1) * chans, so * chans:(so + 1) * chans] = (
                        jnp.zeros((TAPS, chans, chans), bf16))
    edge = jnp.zeros((units, PAD, chans), bf16)
    x_ref[:, 0:PAD, :] = edge
    x_ref[:, PAD + pixels:, :] = edge

    lanes = ANG * SLOT
    col = lax.broadcasted_iota(jnp.int32, (lanes, 2 * ANG), 0)
    chan = lax.broadcasted_iota(jnp.int32, (lanes, 2 * ANG), 1)
    at = SLOT * (chan // 2) + units * lax.rem(chan, 2)
    for u in range(units):
        pick = jnp.where(col == at + u, 1.0, 0.0).astype(bf16)
        spread = jnp.dot(pick, head_t[...], preferred_element_type=f32)
        to = pl.multiple_of((2 * mirrored(u // 2) + u % 2) * chans, chans)
        hb_ref[pl.ds(to, chans), :] = spread.T.astype(bf16)

    line = lax.broadcasted_iota(jnp.int32, (2 * block_rows, bt * SLOT), 0)
    slot = lax.broadcasted_iota(jnp.int32, (2 * block_rows, bt * SLOT), 1)
    part = line // block_rows
    line = line - part * block_rows
    core = line // (block_rows // 2)
    line = line - core * (block_rows // 2)
    tile = line // units
    unit = line - tile * units
    p_ref[...] = jnp.where(
        slot == (2 * tile + core) * SLOT + part * units + unit, 1.0, 0.0).astype(bf16)

    acc_ref[...] = jnp.zeros_like(acc_ref)
    own.wait()
    for copy in w_copies:
        copy.wait()

    def build(p, slot, lo, cw):
        for q in range(2):
            window = x_ref[2 * mirrored(p) + q, pl.ds(lo, cw + 2 * PAD), :]
            for j in range(TAPS):
                first = PAD + 2 * j - (TAPS - 1)
                at = slot * span + j * wide + q * chans
                l_ref[0:cw, at:at + chans] = window[first:first + cw, :]

    def local(c, carry):
        lo = pl.multiple_of(c * BIG, BIG)
        build(0, 0, lo, BIG)
        for p in range(2):
            a_ref[p, pl.ds(lo, BIG), :] = jnp.dot(
                l_ref[:, 0:span], w_ref[1 - p].reshape(span, wide), preferred_element_type=f32)
        return carry

    lax.fori_loop(0, pixels // BIG, local, 0)

    @pl.when(root)
    def _():
        pl.semaphore_wait(barrier, tiles - 1)
        pl.semaphore_signal(all_sem, inc=1, device_id=(1, 0), device_id_type=MESH)

        def tell(i, carry):
            pl.semaphore_signal(all_sem, inc=1, device_id=(0, i), device_id_type=MESH)
            pl.semaphore_signal(all_sem, inc=1, device_id=(1, i), device_id_type=MESH)
            return carry

        lax.fori_loop(1, tiles, tell, 0)

    @pl.when(jnp.logical_not(root))
    def _():
        pl.semaphore_wait(all_sem, 1)

    def near_go(c, lo, cw):
        def source(peer):
            return ns_ref.at[pl.ds(pl.multiple_of(SLOT * (peer // groups), SLOT), SLOT), pl.ds(lo, cw)]

        target = nr_ref.at[pl.ds(pl.multiple_of(SLOT * me, SLOT), SLOT), pl.ds(lo, cw)]

        def send(i, inner):
            peer = lax.rem(me + i, tiles)
            pltpu.make_async_remote_copy(
                src_ref=source(peer), dst_ref=target, send_sem=near_send.at[c],
                recv_sem=near_recv.at[c], device_id=(sec, peer), device_id_type=MESH).start()
            return inner

        lax.fori_loop(1, tiles, send, 0)
        pltpu.make_async_copy(source(me), target, near_recv.at[c]).start()

    def conv(c, lo, cw):
        for p in range(1, pairs):
            build(p, p - 1, lo, cw)
        for p in range(pairs):
            d0, d1 = max(p - 1, 1), min(p + 1, pairs - 1)
            w0, w1 = d0 - p + 1, d1 - p + 2
            pre = jnp.dot(
                l_ref[0:cw, (d0 - 1) * span:d1 * span],
                w_ref[w0:w1].reshape((w1 - w0) * span, wide),
                preferred_element_type=f32)
            if p < 2:
                pre += a_ref[p, pl.ds(lo, cw), :]
            h_ref[0:cw, p * wide:(p + 1) * wide] = jax.nn.gelu(pre, approximate=True).astype(bf16)
        near = jnp.dot(h_ref[0:cw, :], hb_ref[...], preferred_element_type=f32)
        ns_ref[:, pl.ds(lo, cw)] = near.T.astype(bf16)
        near_go(c, lo, cw)

    def gather(c, lo, cw):
        arrived = nr_ref.at[:, pl.ds(lo, cw)]
        pltpu.make_async_copy(arrived, arrived, near_recv.at[c]).wait()
        for b in range(tiles // bt):
            field = jnp.dot(
                p_ref[...], nr_ref[b * bt * SLOT:(b + 1) * bt * SLOT, pl.ds(lo, cw)],
                preferred_element_type=f32).astype(bf16)
            for core in range(2):
                n = block_rows // 2
                real = field[core * n:(core + 1) * n]
                imag = field[block_rows + core * n:block_rows + (core + 1) * n]
                at = core * side_rows + b * n
                e_ref[at:at + n, 0:cw] = real
                e_ref[rows + at:rows + at + n, 0:cw] = imag
                e_ref[at:at + n, cw:2 * cw] = -imag
                e_ref[rows + at:rows + at + n, cw:2 * cw] = real

    def product(lo, cw, v, k):
        at = v * vw
        if cw < BIG:
            both = jnp.concatenate(
                [g_ref[k, pl.ds(lo, cw), at:at + vw],
                 g_ref[k, pl.ds(lo, cw), pixels + at:pixels + at + vw]], axis=0)
            return jnp.dot(e_ref[:, 0:2 * cw], both, preferred_element_type=f32)
        amp = jnp.dot(e_ref[:, 0:cw], g_ref[k, pl.ds(lo, cw), at:at + vw],
                      preferred_element_type=f32)
        return amp + jnp.dot(e_ref[:, cw:2 * cw],
                             g_ref[k, pl.ds(lo, cw), pixels + at:pixels + at + vw],
                             preferred_element_type=f32)

    def images(lo, cw):
        def image(kb, inner):
            for i in range(unroll):
                for v in range(part_v):
                    acc_ref[kb * unroll + i, v] += product(lo, cw, v, kb * unroll + i)
            return inner

        lax.fori_loop(0, kers // unroll, image, 0)

    def step(c, carry):
        for cc in range(bigs):
            @pl.when(c == cc)
            def _():
                halos[cc].wait_recv()

        @pl.when(c < bigs)
        def _():
            conv(c, pl.multiple_of(c * BIG, BIG), BIG)

        @pl.when(c == bigs)
        def _():
            def small(s, inner):
                for ss in range(SMALLS):
                    @pl.when(s == ss)
                    def _():
                        halos[bigs + ss].wait_recv()
                conv(bigs + s, pl.multiple_of(bigs * BIG + s * SMALL, SMALL), SMALL)
                return inner

            lax.fori_loop(0, SMALLS, small, 0)

        @pl.when(c == 1)
        def _():
            for copy in g_copies:
                copy.wait()

        @pl.when(c > 0)
        def _():
            lo = pl.multiple_of((c - 1) * BIG, BIG)
            gather(c - 1, lo, BIG)
            images(lo, BIG)

        return carry

    lax.fori_loop(0, bigs + 1, step, 0)
    for c in range(bigs, chunks - 1):
        gather(c, edges[c], SMALL)
        images(edges[c], SMALL)
    gather(chunks - 1, edges[-2], SMALL)

    weight = source_w[me // groups]
    chip = me // 2
    chips = tiles // 2

    def ret_copy(n, h, i):
        return pltpu.make_async_remote_copy(
            src_ref=r_ref.at[n, i, h], dst_ref=rr_ref.at[n, sec, chip],
            send_sem=ret_send.at[n], recv_sem=ret_recv.at[n],
            device_id=(h, 2 * i + side), device_id_type=MESH)

    cx_copies = []

    def ret_block(n):
        cx_copies[n].wait_recv()
        mine = s_ref[pl.ds(pl.multiple_of(side * side_rows, 16), side_rows), n * pw:(n + 1) * pw]
        mine = mine + cx_ref[n]
        for i in range(chips):
            for h in range(2):
                first = i * units + h * half
                r_ref[n, i, h] = mine[first:first + half].astype(bf16)

        def ret_go(i, carry):
            peer = lax.rem(chip + i, chips)
            ret_copy(n, sec, peer).start()
            ret_copy(n, 1 - sec, peer).start()
            return carry

        lax.fori_loop(1, chips, ret_go, 0)
        ret_copy(n, 1 - sec, chip).start()
        pltpu.make_async_copy(r_ref.at[n, chip, sec], rr_ref.at[n, sec, chip], ret_recv.at[n]).start()

    for n in range(SENDS):
        for m in range(per_send):
            v = n * per_send + m

            def power(kb, total):
                for i in range(unroll):
                    k = kb * unroll + i
                    amp = acc_ref[k, v] + product(edges[-2], SMALL, v, k)
                    square = amp * amp
                    total = total + (square[0:rows] + square[rows:])
                return total

            total = jnp.zeros((rows, vw), f32)
            if kers == unroll:
                total = power(0, total)
            else:
                total = lax.fori_loop(0, kers // unroll, power, total)
            s_ref[:, v * vw:(v + 1) * vw] = total * weight
        copy = pltpu.make_async_remote_copy(
            src_ref=s_ref.at[pl.ds(pl.multiple_of((1 - side) * side_rows, 16), side_rows),
                             pl.ds(n * pw, pw)],
            dst_ref=cx_ref.at[n], send_sem=cx_send.at[n], recv_sem=cx_recv.at[n],
            device_id=(sec, sibling), device_id_type=MESH)
        copy.start()
        cx_copies.append(copy)
        if n:
            ret_block(n - 1)
    ret_block(SENDS - 1)

    for n in range(SENDS):
        pltpu.make_async_copy(rr_ref.at[n], rr_ref.at[n], ret_recv.at[n]).wait()
        for par in range(2):
            total = rr_ref[n, par, 0].astype(f32)
            for i in range(1, chips):
                total = total + rr_ref[n, par, i].astype(f32)
            for j in range(half):
                out_ref[0, 2 * j + par:2 * j + par + 1, n * pw:(n + 1) * pw] = total[j:j + 1]

    sent = feat.at[:, sec]
    pltpu.make_async_copy(sent, sent, halo_send).wait()
    for c in range(chunks):
        sent = nr_ref.at[pl.ds(0, (tiles - 1) * SLOT), pl.ds(edges[c], edges[c + 1] - edges[c])]
        pltpu.make_async_copy(sent, sent, near_send.at[c]).wait()
    for n in range(SENDS):
        cx_copies[n].wait_send()

        def ret_sent(i, carry):
            ret_copy(n, sec, 0).wait_send()
            ret_copy(n, 1 - sec, 0).wait_send()
            return carry

        lax.fori_loop(1, chips, ret_sent, 0)
        ret_copy(n, 1 - sec, 0).wait_send()


def on_device(features, conv_weight, head_weight, kernels, source_weights):
    tiles = lax.axis_size("tile")
    groups = tiles // ANG
    _, rows_dev, pixels, chans = features.shape
    half = rows_dev // 2
    units = 2 * half
    kers = kernels.shape[0]
    rows = tiles * units
    bt = min(tiles, 16)
    chunks = (pixels - SMALLS * SMALL) // BIG + SMALLS
    bf16, f32 = jnp.bfloat16, jnp.float32
    feat = features.reshape(half, 2, pixels, chans)
    any_spec = pl.BlockSpec(memory_space=pl.ANY)
    image = pl.pallas_call(
        functools.partial(kernel, tiles, groups),
        out_shape=jax.ShapeDtypeStruct((1, rows_dev, pixels), f32),
        in_specs=[
            any_spec,
            any_spec,
            pl.BlockSpec(memory_space=pltpu.VMEM),
            any_spec,
            pl.BlockSpec(memory_space=pltpu.SMEM),
        ],
        out_specs=pl.BlockSpec(memory_space=pltpu.VMEM),
        scratch_shapes=[
            pltpu.VMEM((units, pixels + 2 * PAD, chans), bf16),
            pltpu.VMEM((3, TAPS, 2 * chans, 2 * chans), bf16),
            pltpu.VMEM((BIG, (units // 2 - 1) * TAPS * 2 * chans), bf16),
            pltpu.VMEM((2, pixels, 2 * chans), f32),
            pltpu.VMEM((BIG, units * chans), bf16),
            pltpu.VMEM((units * chans, ANG * SLOT), bf16),
            pltpu.VMEM((2 * bt * units, bt * SLOT), bf16),
            pltpu.VMEM((ANG * SLOT, pixels), bf16),
            pltpu.VMEM((tiles * SLOT, pixels), bf16),
            pltpu.VMEM((2 * rows, 2 * BIG), bf16),
            pltpu.VMEM((kers, pixels // 256, 2 * rows, 256), f32),
            pltpu.VMEM((kers, pixels, 2 * pixels), bf16),
            pltpu.VMEM((rows, pixels), f32),
            pltpu.VMEM((SENDS, rows // 2, pixels // SENDS), f32),
            pltpu.VMEM((SENDS, tiles // 2, 2, half, pixels // SENDS), bf16),
            pltpu.VMEM((SENDS, 2, tiles // 2, half, pixels // SENDS), bf16),
            pltpu.SemaphoreType.DMA,
            pltpu.SemaphoreType.DMA((10,)),
            pltpu.SemaphoreType.DMA((kers,)),
            pltpu.SemaphoreType.DMA,
            pltpu.SemaphoreType.DMA((chunks,)),
            pltpu.SemaphoreType.DMA((chunks,)),
            pltpu.SemaphoreType.DMA((chunks,)),
            pltpu.SemaphoreType.DMA((SENDS,)),
            pltpu.SemaphoreType.DMA((SENDS,)),
            pltpu.SemaphoreType.DMA((SENDS,)),
            pltpu.SemaphoreType.DMA((SENDS,)),
            pltpu.SemaphoreType.REGULAR,
            pltpu.SemaphoreType.REGULAR,
        ],
        compiler_params=pltpu.CompilerParams(
            collective_id=0, has_side_effects=True, vmem_limit_bytes=66_000_000),
    )(feat, conv_weight, head_weight.T, kernels, source_weights)
    return image


def solution(mesh):
    in_specs = (P("tile", "section", None, None), P(), P(), P("tile", None, None), P())
    out_specs = P("tile", "section", None)
    return jax.shard_map(
        on_device, mesh=mesh, in_specs=in_specs, out_specs=out_specs, check_vma=False
    )
```

```python
import functools

import jax
import jax.numpy as jnp
from jax import lax
from jax.experimental import pallas as pl
from jax.experimental.pallas import tpu as pltpu
from jax.sharding import PartitionSpec as P

ANG = 8
TAPS = 5
BIG = 256
SMALL = 128
SMALLS = 2
PAD = 16
SLOT = 16
SENDS = 1
MESH = pl.DeviceIdType.MESH


def kernel(tiles, groups, feat, conv_w, head_t, operators, source_w, rr_ref,
           x_ref, w_ref, l_ref, a_ref, h_ref, hb_ref, p_ref, ns_ref, nr_ref, e_ref, acc_ref, g_ref,
           s_ref, cx_ref, r_ref,
           own_sem, w_sem, g_sem, halo_send, halo_recv, near_send, near_recv,
           cx_send, cx_recv, ret_send, ret_recv, met_sem, all_sem):
    bf16, f32 = jnp.bfloat16, jnp.float32
    sec = lax.axis_index("section")
    me = lax.axis_index("tile")
    side = lax.rem(me, 2)
    sibling = me + 1 - 2 * side
    half, pixels, chans = feat.shape[0], feat.shape[2], feat.shape[3]
    units = 2 * half
    pairs = units // 2
    kers = operators.shape[0]
    bigs = (pixels - SMALLS * SMALL) // BIG
    edges = [c * BIG for c in range(bigs)] + [bigs * BIG + s * SMALL for s in range(SMALLS)] + [pixels]
    chunks = len(edges) - 1
    span = TAPS * 2 * chans
    wide = 2 * chans
    rows = tiles * units
    side_rows = rows // 2
    bt = min(tiles, 16)
    block_rows = bt * units
    vw = 256
    part_v = pixels // vw
    per_send = part_v // SENDS
    pw = pixels // SENDS
    unroll = min(kers, 8)

    barrier = pltpu.get_barrier_semaphore()
    root = jnp.logical_and(me == 0, sec == 0)
    beside = jnp.logical_and(me == 0, sec == 1)

    @pl.when(jnp.logical_not(beside))
    def _():
        pl.semaphore_signal(barrier, inc=1, device_id=(1 - sec, me), device_id_type=MESH)

    def mirrored(i):
        return i + sec * (pairs - 1 - 2 * i)

    own = pltpu.make_async_copy(
        feat.at[:, sec], x_ref.at[pl.ds(sec * half, half), pl.ds(PAD, pixels), :], own_sem)
    own.start()
    w_copies = []
    for d in range(3):
        for si in range(2):
            for so in range(2):
                tap = 2 * d + si - so
                if 0 <= tap < TAPS:
                    copy = pltpu.make_async_copy(
                        conv_w.at[tap],
                        w_ref.at[mirrored(d), :, pl.ds(si * chans, chans), pl.ds(so * chans, chans)],
                        w_sem.at[len(w_copies)])
                    copy.start()
                    w_copies.append(copy)

    @pl.when(jnp.logical_not(root))
    def _():
        pl.semaphore_wait(barrier, 1)

    @pl.when(beside)
    def _():
        pl.semaphore_signal(met_sem, inc=1, device_id=(0, 0), device_id_type=MESH)

    @pl.when(root)
    def _():
        pl.semaphore_wait(met_sem, 1)

    halos = []
    for c in range(chunks):
        lo = 0 if c == 0 else edges[c] + PAD
        hi = pixels if c == chunks - 1 else edges[c + 1] + PAD
        copy = pltpu.make_async_remote_copy(
            src_ref=feat.at[:, 1 - sec, pl.ds(lo, hi - lo), :],
            dst_ref=x_ref.at[pl.ds(sec * half, half), pl.ds(PAD + lo, hi - lo), :],
            send_sem=halo_send, recv_sem=halo_recv.at[c],
            device_id=(1 - sec, me), device_id_type=MESH)
        copy.start()
        halos.append(copy)

    @pl.when(jnp.logical_and(me > 0, sec == 0))
    def _():
        pl.semaphore_signal(barrier, inc=1, device_id=(0, 0), device_id_type=MESH)

    g_copies = []
    for k in range(kers):
        copy = pltpu.make_async_copy(operators.at[k], g_ref.at[k], g_sem.at[k])
        copy.start()
        g_copies.append(copy)

    for d in range(3):
        for si in range(2):
            for so in range(2):
                if not 0 <= 2 * d + si - so < TAPS:
                    w_ref[mirrored(d), :, si * chans:(si + 1) * chans, so * chans:(so + 1) * chans] = (
                        jnp.zeros((TAPS, chans, chans), bf16))
    edge = jnp.zeros((units, PAD, chans), bf16)
    x_ref[:, 0:PAD, :] = edge
    x_ref[:, PAD + pixels:, :] = edge

    lanes = ANG * SLOT
    col = lax.broadcasted_iota(jnp.int32, (lanes, 2 * ANG), 0)
    chan = lax.broadcasted_iota(jnp.int32, (lanes, 2 * ANG), 1)
    at = SLOT * (chan // 2) + units * lax.rem(chan, 2)
    for u in range(units):
        pick = jnp.where(col == at + u, 1.0, 0.0).astype(bf16)
        spread = jnp.dot(pick, head_t[...], preferred_element_type=f32)
        to = pl.multiple_of((2 * mirrored(u // 2) + u % 2) * chans, chans)
        hb_ref[pl.ds(to, chans), :] = spread.T.astype(bf16)

    line = lax.broadcasted_iota(jnp.int32, (2 * block_rows, bt * SLOT), 0)
    slot = lax.broadcasted_iota(jnp.int32, (2 * block_rows, bt * SLOT), 1)
    part = line // block_rows
    line = line - part * block_rows
    core = line // (block_rows // 2)
    line = line - core * (block_rows // 2)
    tile = line // units
    unit = line - tile * units
    p_ref[...] = jnp.where(
        slot == (2 * tile + core) * SLOT + part * units + unit, 1.0, 0.0).astype(bf16)

    acc_ref[...] = jnp.zeros_like(acc_ref)
    own.wait()
    for copy in w_copies:
        copy.wait()

    def build(p, slot, lo, cw):
        for q in range(2):
            window = x_ref[2 * mirrored(p) + q, pl.ds(lo, cw + 2 * PAD), :]
            for j in range(TAPS):
                first = PAD + 2 * j - (TAPS - 1)
                at = slot * span + j * wide + q * chans
                l_ref[0:cw, at:at + chans] = window[first:first + cw, :]

    def local(c, carry):
        lo = pl.multiple_of(c * BIG, BIG)
        build(0, 0, lo, BIG)
        for p in range(2):
            a_ref[p, pl.ds(lo, BIG), :] = jnp.dot(
                l_ref[:, 0:span], w_ref[1 - p].reshape(span, wide), preferred_element_type=f32)
        return carry

    lax.fori_loop(0, pixels // BIG, local, 0)

    @pl.when(root)
    def _():
        pl.semaphore_wait(barrier, tiles - 1)
        pl.semaphore_signal(all_sem, inc=1, device_id=(1, 0), device_id_type=MESH)

        def tell(i, carry):
            pl.semaphore_signal(all_sem, inc=1, device_id=(0, i), device_id_type=MESH)
            pl.semaphore_signal(all_sem, inc=1, device_id=(1, i), device_id_type=MESH)
            return carry

        lax.fori_loop(1, tiles, tell, 0)

    @pl.when(jnp.logical_not(root))
    def _():
        pl.semaphore_wait(all_sem, 1)

    def near_go(c, lo, cw):
        def source(peer):
            return ns_ref.at[pl.ds(pl.multiple_of(SLOT * (peer // groups), SLOT), SLOT), pl.ds(lo, cw)]

        target = nr_ref.at[pl.ds(pl.multiple_of(SLOT * me, SLOT), SLOT), pl.ds(lo, cw)]

        def send(i, inner):
            peer = lax.rem(me + i, tiles)
            pltpu.make_async_remote_copy(
                src_ref=source(peer), dst_ref=target, send_sem=near_send.at[c],
                recv_sem=near_recv.at[c], device_id=(sec, peer), device_id_type=MESH).start()
            return inner

        lax.fori_loop(1, tiles, send, 0)
        pltpu.make_async_copy(source(me), target, near_recv.at[c]).start()

    def conv(c, lo, cw):
        for p in range(1, pairs):
            build(p, p - 1, lo, cw)
        for p in range(pairs):
            d0, d1 = max(p - 1, 1), min(p + 1, pairs - 1)
            w0, w1 = d0 - p + 1, d1 - p + 2
            pre = jnp.dot(
                l_ref[0:cw, (d0 - 1) * span:d1 * span],
                w_ref[w0:w1].reshape((w1 - w0) * span, wide),
                preferred_element_type=f32)
            if p < 2:
                pre += a_ref[p, pl.ds(lo, cw), :]
            h_ref[0:cw, p * wide:(p + 1) * wide] = jax.nn.gelu(pre, approximate=True).astype(bf16)
        near = jnp.dot(h_ref[0:cw, :], hb_ref[...], preferred_element_type=f32)
        ns_ref[:, pl.ds(lo, cw)] = near.T.astype(bf16)
        near_go(c, lo, cw)

    def gather(c, lo, cw):
        arrived = nr_ref.at[:, pl.ds(lo, cw)]
        pltpu.make_async_copy(arrived, arrived, near_recv.at[c]).wait()
        for b in range(tiles // bt):
            field = jnp.dot(
                p_ref[...], nr_ref[b * bt * SLOT:(b + 1) * bt * SLOT, pl.ds(lo, cw)],
                preferred_element_type=f32).astype(bf16)
            for core in range(2):
                n = block_rows // 2
                real = field[core * n:(core + 1) * n]
                imag = field[block_rows + core * n:block_rows + (core + 1) * n]
                at = core * side_rows + b * n
                e_ref[at:at + n, 0:cw] = real
                e_ref[rows + at:rows + at + n, 0:cw] = imag
                e_ref[at:at + n, cw:2 * cw] = -imag
                e_ref[rows + at:rows + at + n, cw:2 * cw] = real

    def product(lo, cw, v, k):
        at = v * vw
        if cw < BIG:
            both = jnp.concatenate(
                [g_ref[k, pl.ds(lo, cw), at:at + vw],
                 g_ref[k, pl.ds(lo, cw), pixels + at:pixels + at + vw]], axis=0)
            return jnp.dot(e_ref[:, 0:2 * cw], both, preferred_element_type=f32)
        amp = jnp.dot(e_ref[:, 0:cw], g_ref[k, pl.ds(lo, cw), at:at + vw],
                      preferred_element_type=f32)
        return amp + jnp.dot(e_ref[:, cw:2 * cw],
                             g_ref[k, pl.ds(lo, cw), pixels + at:pixels + at + vw],
                             preferred_element_type=f32)

    def images(lo, cw):
        def image(kb, inner):
            for i in range(unroll):
                for v in range(part_v):
                    acc_ref[kb * unroll + i, v] += product(lo, cw, v, kb * unroll + i)
            return inner

        lax.fori_loop(0, kers // unroll, image, 0)

    def step(c, carry):
        for cc in range(bigs):
            @pl.when(c == cc)
            def _():
                halos[cc].wait_recv()

        @pl.when(c < bigs)
        def _():
            conv(c, pl.multiple_of(c * BIG, BIG), BIG)

        @pl.when(c == bigs)
        def _():
            def small(s, inner):
                for ss in range(SMALLS):
                    @pl.when(s == ss)
                    def _():
                        halos[bigs + ss].wait_recv()
                conv(bigs + s, pl.multiple_of(bigs * BIG + s * SMALL, SMALL), SMALL)
                return inner

            lax.fori_loop(0, SMALLS, small, 0)

        @pl.when(c == 1)
        def _():
            for copy in g_copies:
                copy.wait()

        @pl.when(c > 0)
        def _():
            lo = pl.multiple_of((c - 1) * BIG, BIG)
            gather(c - 1, lo, BIG)
            images(lo, BIG)

        return carry

    lax.fori_loop(0, bigs + 1, step, 0)
    for c in range(bigs, chunks - 1):
        gather(c, edges[c], SMALL)
        images(edges[c], SMALL)
    gather(chunks - 1, edges[-2], SMALL)

    weight = source_w[me // groups]
    chip = me // 2
    chips = tiles // 2

    def ret_copy(n, h, i):
        return pltpu.make_async_remote_copy(
            src_ref=r_ref.at[n, i, h], dst_ref=rr_ref.at[n, sec, chip],
            send_sem=ret_send.at[n], recv_sem=ret_recv.at[n],
            device_id=(h, 2 * i + side), device_id_type=MESH)

    cx_copies = []

    def ret_block(n):
        cx_copies[n].wait_recv()
        mine = s_ref[pl.ds(pl.multiple_of(side * side_rows, 16), side_rows), n * pw:(n + 1) * pw]
        mine = mine + cx_ref[n]
        for i in range(chips):
            for h in range(2):
                first = i * units + h * half
                r_ref[n, i, h] = mine[first:first + half].astype(bf16)

        def ret_go(i, carry):
            peer = lax.rem(chip + i, chips)
            ret_copy(n, sec, peer).start()
            ret_copy(n, 1 - sec, peer).start()
            return carry

        lax.fori_loop(1, chips, ret_go, 0)
        ret_copy(n, 1 - sec, chip).start()
        pltpu.make_async_copy(r_ref.at[n, chip, sec], rr_ref.at[n, sec, chip], ret_recv.at[n]).start()

    for n in range(SENDS):
        for m in range(per_send):
            v = n * per_send + m

            def power(kb, total):
                for i in range(unroll):
                    k = kb * unroll + i
                    amp = acc_ref[k, v] + product(edges[-2], SMALL, v, k)
                    square = amp * amp
                    total = total + (square[0:rows] + square[rows:])
                return total

            total = jnp.zeros((rows, vw), f32)
            if kers == unroll:
                total = power(0, total)
            else:
                total = lax.fori_loop(0, kers // unroll, power, total)
            s_ref[:, v * vw:(v + 1) * vw] = total * weight
        copy = pltpu.make_async_remote_copy(
            src_ref=s_ref.at[pl.ds(pl.multiple_of((1 - side) * side_rows, 16), side_rows),
                             pl.ds(n * pw, pw)],
            dst_ref=cx_ref.at[n], send_sem=cx_send.at[n], recv_sem=cx_recv.at[n],
            device_id=(sec, sibling), device_id_type=MESH)
        copy.start()
        cx_copies.append(copy)
        if n:
            ret_block(n - 1)
    ret_block(SENDS - 1)

    for n in range(SENDS):
        pltpu.make_async_copy(rr_ref.at[n], rr_ref.at[n], ret_recv.at[n]).wait()

    sent = feat.at[:, sec]
    pltpu.make_async_copy(sent, sent, halo_send).wait()
    for c in range(chunks):
        sent = nr_ref.at[pl.ds(0, (tiles - 1) * SLOT), pl.ds(edges[c], edges[c + 1] - edges[c])]
        pltpu.make_async_copy(sent, sent, near_send.at[c]).wait()
    for n in range(SENDS):
        cx_copies[n].wait_send()

        def ret_sent(i, carry):
            ret_copy(n, sec, 0).wait_send()
            ret_copy(n, 1 - sec, 0).wait_send()
            return carry

        lax.fori_loop(1, chips, ret_sent, 0)
        ret_copy(n, 1 - sec, 0).wait_send()


def on_device(features, conv_weight, head_weight, kernels, source_weights):
    tiles = lax.axis_size("tile")
    groups = tiles // ANG
    _, rows_dev, pixels, chans = features.shape
    half = rows_dev // 2
    units = 2 * half
    kers = kernels.shape[0]
    rows = tiles * units
    bt = min(tiles, 16)
    chunks = (pixels - SMALLS * SMALL) // BIG + SMALLS
    bf16, f32 = jnp.bfloat16, jnp.float32
    feat = features.reshape(half, 2, pixels, chans)
    any_spec = pl.BlockSpec(memory_space=pl.ANY)
    arrived = pl.pallas_call(
        functools.partial(kernel, tiles, groups),
        out_shape=jax.ShapeDtypeStruct((SENDS, 2, tiles // 2, half, pixels // SENDS), bf16),
        in_specs=[
            any_spec,
            any_spec,
            pl.BlockSpec(memory_space=pltpu.VMEM),
            any_spec,
            pl.BlockSpec(memory_space=pltpu.SMEM),
        ],
        out_specs=pl.BlockSpec(memory_space=pl.ANY),
        scratch_shapes=[
            pltpu.VMEM((units, pixels + 2 * PAD, chans), bf16),
            pltpu.VMEM((3, TAPS, 2 * chans, 2 * chans), bf16),
            pltpu.VMEM((BIG, (units // 2 - 1) * TAPS * 2 * chans), bf16),
            pltpu.VMEM((2, pixels, 2 * chans), f32),
            pltpu.VMEM((BIG, units * chans), bf16),
            pltpu.VMEM((units * chans, ANG * SLOT), bf16),
            pltpu.VMEM((2 * bt * units, bt * SLOT), bf16),
            pltpu.VMEM((ANG * SLOT, pixels), bf16),
            pltpu.VMEM((tiles * SLOT, pixels), bf16),
            pltpu.VMEM((2 * rows, 2 * BIG), bf16),
            pltpu.VMEM((kers, pixels // 256, 2 * rows, 256), f32),
            pltpu.VMEM((kers, pixels, 2 * pixels), bf16),
            pltpu.VMEM((rows, pixels), f32),
            pltpu.VMEM((SENDS, rows // 2, pixels // SENDS), f32),
            pltpu.VMEM((SENDS, tiles // 2, 2, half, pixels // SENDS), bf16),
            pltpu.SemaphoreType.DMA,
            pltpu.SemaphoreType.DMA((10,)),
            pltpu.SemaphoreType.DMA((kers,)),
            pltpu.SemaphoreType.DMA,
            pltpu.SemaphoreType.DMA((chunks,)),
            pltpu.SemaphoreType.DMA((chunks,)),
            pltpu.SemaphoreType.DMA((chunks,)),
            pltpu.SemaphoreType.DMA((SENDS,)),
            pltpu.SemaphoreType.DMA((SENDS,)),
            pltpu.SemaphoreType.DMA((SENDS,)),
            pltpu.SemaphoreType.DMA((SENDS,)),
            pltpu.SemaphoreType.REGULAR,
            pltpu.SemaphoreType.REGULAR,
        ],
        compiler_params=pltpu.CompilerParams(
            collective_id=0, has_side_effects=True, vmem_limit_bytes=66_000_000),
    )(feat, conv_weight, head_weight.T, kernels, source_weights)
    image = jnp.sum(arrived.astype(f32), axis=2)
    return image.transpose(2, 1, 0, 3).reshape(1, rows_dev, pixels)


def solution(mesh):
    in_specs = (P("tile", "section", None, None), P(), P(), P("tile", None, None), P())
    out_specs = P("tile", "section", None)
    return jax.shard_map(
        on_device, mesh=mesh, in_specs=in_specs, out_specs=out_specs, check_vma=False
    )
```

```python
import functools

import jax
import jax.numpy as jnp
from jax import lax
from jax.experimental import pallas as pl
from jax.experimental.pallas import tpu as pltpu
from jax.sharding import PartitionSpec as P

ANG = 8
TAPS = 5
BIG = 256
SMALL = 128
SMALLS = 2
PAD = 16
SLOT = 16
SENDS = 1
MESH = pl.DeviceIdType.MESH


def kernel(tiles, groups, feat, conv_w, head_t, operators, source_w, rr_ref,
           x_ref, w_ref, l_ref, a_ref, h_ref, hb_ref, p_ref, ns_ref, nr_ref, e_ref, acc_ref, g_ref,
           s_ref, cx_ref, r_ref,
           own_sem, w_sem, g_sem, halo_send, halo_recv, near_send, near_recv,
           cx_send, cx_recv, ret_send, ret_recv, met_sem, all_sem):
    bf16, f32 = jnp.bfloat16, jnp.float32
    sec = lax.axis_index("section")
    me = lax.axis_index("tile")
    side = lax.rem(me, 2)
    sibling = me + 1 - 2 * side
    half, pixels, chans = feat.shape[0], feat.shape[2], feat.shape[3]
    units = 2 * half
    pairs = units // 2
    kers = operators.shape[0]
    bigs = (pixels - SMALLS * SMALL) // BIG
    edges = [c * BIG for c in range(bigs)] + [bigs * BIG + s * SMALL for s in range(SMALLS)] + [pixels]
    chunks = len(edges) - 1
    span = TAPS * 2 * chans
    wide = 2 * chans
    rows = tiles * units
    side_rows = rows // 2
    bt = min(tiles, 16)
    block_rows = bt * units
    vw = 256
    part_v = pixels // vw
    per_send = part_v // SENDS
    pw = pixels // SENDS
    unroll = min(kers, 8)

    barrier = pltpu.get_barrier_semaphore()
    root = jnp.logical_and(me == 0, sec == 0)
    beside = jnp.logical_and(me == 0, sec == 1)

    @pl.when(jnp.logical_not(beside))
    def _():
        pl.semaphore_signal(barrier, inc=1, device_id=(1 - sec, me), device_id_type=MESH)

    def mirrored(i):
        return i + sec * (pairs - 1 - 2 * i)

    own = pltpu.make_async_copy(
        feat.at[:, sec], x_ref.at[pl.ds(sec * half, half), pl.ds(PAD, pixels), :], own_sem)
    own.start()
    w_copies = []
    for d in range(3):
        for si in range(2):
            for so in range(2):
                tap = 2 * d + si - so
                if 0 <= tap < TAPS:
                    copy = pltpu.make_async_copy(
                        conv_w.at[tap],
                        w_ref.at[mirrored(d), :, pl.ds(si * chans, chans), pl.ds(so * chans, chans)],
                        w_sem.at[len(w_copies)])
                    copy.start()
                    w_copies.append(copy)

    @pl.when(jnp.logical_not(root))
    def _():
        pl.semaphore_wait(barrier, 1)

    @pl.when(beside)
    def _():
        pl.semaphore_signal(met_sem, inc=1, device_id=(0, 0), device_id_type=MESH)

    @pl.when(root)
    def _():
        pl.semaphore_wait(met_sem, 1)

    halos = []
    for c in range(chunks):
        lo = 0 if c == 0 else edges[c] + PAD
        hi = pixels if c == chunks - 1 else edges[c + 1] + PAD
        copy = pltpu.make_async_remote_copy(
            src_ref=feat.at[:, 1 - sec, pl.ds(lo, hi - lo), :],
            dst_ref=x_ref.at[pl.ds(sec * half, half), pl.ds(PAD + lo, hi - lo), :],
            send_sem=halo_send, recv_sem=halo_recv.at[c],
            device_id=(1 - sec, me), device_id_type=MESH)
        copy.start()
        halos.append(copy)

    @pl.when(jnp.logical_and(me > 0, sec == 0))
    def _():
        pl.semaphore_signal(barrier, inc=1, device_id=(0, 0), device_id_type=MESH)

    g_copies = []
    for k in range(kers):
        copy = pltpu.make_async_copy(operators.at[k], g_ref.at[k], g_sem.at[k])
        copy.start()
        g_copies.append(copy)

    for d in range(3):
        for si in range(2):
            for so in range(2):
                if not 0 <= 2 * d + si - so < TAPS:
                    w_ref[mirrored(d), :, si * chans:(si + 1) * chans, so * chans:(so + 1) * chans] = (
                        jnp.zeros((TAPS, chans, chans), bf16))
    edge = jnp.zeros((units, PAD, chans), bf16)
    x_ref[:, 0:PAD, :] = edge
    x_ref[:, PAD + pixels:, :] = edge

    lanes = ANG * SLOT
    col = lax.broadcasted_iota(jnp.int32, (lanes, 2 * ANG), 0)
    chan = lax.broadcasted_iota(jnp.int32, (lanes, 2 * ANG), 1)
    at = SLOT * (chan // 2) + units * lax.rem(chan, 2)
    for u in range(units):
        pick = jnp.where(col == at + u, 1.0, 0.0).astype(bf16)
        spread = jnp.dot(pick, head_t[...], preferred_element_type=f32)
        to = pl.multiple_of((2 * mirrored(u // 2) + u % 2) * chans, chans)
        hb_ref[pl.ds(to, chans), :] = spread.T.astype(bf16)

    line = lax.broadcasted_iota(jnp.int32, (2 * block_rows, bt * SLOT), 0)
    slot = lax.broadcasted_iota(jnp.int32, (2 * block_rows, bt * SLOT), 1)
    part = line // block_rows
    line = line - part * block_rows
    core = line // (block_rows // 2)
    line = line - core * (block_rows // 2)
    tile = line // units
    unit = line - tile * units
    p_ref[...] = jnp.where(
        slot == (2 * tile + core) * SLOT + part * units + unit, 1.0, 0.0).astype(bf16)

    acc_ref[...] = jnp.zeros_like(acc_ref)
    own.wait()
    for copy in w_copies:
        copy.wait()

    def build(p, slot, lo, cw):
        for q in range(2):
            window = x_ref[2 * mirrored(p) + q, pl.ds(lo, cw + 2 * PAD), :]
            for j in range(TAPS):
                first = PAD + 2 * j - (TAPS - 1)
                at = slot * span + j * wide + q * chans
                l_ref[0:cw, at:at + chans] = window[first:first + cw, :]

    def local(c, carry):
        lo = pl.multiple_of(c * BIG, BIG)
        build(0, 0, lo, BIG)
        for p in range(2):
            a_ref[p, pl.ds(lo, BIG), :] = jnp.dot(
                l_ref[:, 0:span], w_ref[1 - p].reshape(span, wide), preferred_element_type=f32)
        return carry

    lax.fori_loop(0, pixels // BIG, local, 0)

    @pl.when(root)
    def _():
        pl.semaphore_wait(barrier, tiles - 1)
        pl.semaphore_signal(all_sem, inc=1, device_id=(1, 0), device_id_type=MESH)

        def tell(i, carry):
            pl.semaphore_signal(all_sem, inc=1, device_id=(0, i), device_id_type=MESH)
            pl.semaphore_signal(all_sem, inc=1, device_id=(1, i), device_id_type=MESH)
            return carry

        lax.fori_loop(1, tiles, tell, 0)

    @pl.when(jnp.logical_not(root))
    def _():
        pl.semaphore_wait(all_sem, 1)

    def near_go(c, lo, cw):
        def source(peer):
            return ns_ref.at[pl.ds(pl.multiple_of(SLOT * (peer // groups), SLOT), SLOT), pl.ds(lo, cw)]

        target = nr_ref.at[pl.ds(pl.multiple_of(SLOT * me, SLOT), SLOT), pl.ds(lo, cw)]

        def send(i, inner):
            peer = lax.rem(me + i, tiles)
            pltpu.make_async_remote_copy(
                src_ref=source(peer), dst_ref=target, send_sem=near_send.at[c],
                recv_sem=near_recv.at[c], device_id=(sec, peer), device_id_type=MESH).start()
            return inner

        lax.fori_loop(1, tiles, send, 0, unroll=5 if tiles == 16 else 1)
        pltpu.make_async_copy(source(me), target, near_recv.at[c]).start()

    def conv(c, lo, cw):
        for p in range(1, pairs):
            build(p, p - 1, lo, cw)
        for p in range(pairs):
            d0, d1 = max(p - 1, 1), min(p + 1, pairs - 1)
            w0, w1 = d0 - p + 1, d1 - p + 2
            pre = jnp.dot(
                l_ref[0:cw, (d0 - 1) * span:d1 * span],
                w_ref[w0:w1].reshape((w1 - w0) * span, wide),
                preferred_element_type=f32)
            if p < 2:
                pre += a_ref[p, pl.ds(lo, cw), :]
            h_ref[0:cw, p * wide:(p + 1) * wide] = jax.nn.gelu(pre, approximate=True).astype(bf16)
        near = jnp.dot(h_ref[0:cw, :], hb_ref[...], preferred_element_type=f32)
        ns_ref[:, pl.ds(lo, cw)] = near.T.astype(bf16)
        near_go(c, lo, cw)

    def gather(c, lo, cw):
        arrived = nr_ref.at[:, pl.ds(lo, cw)]
        pltpu.make_async_copy(arrived, arrived, near_recv.at[c]).wait()
        for b in range(tiles // bt):
            field = jnp.dot(
                p_ref[...], nr_ref[b * bt * SLOT:(b + 1) * bt * SLOT, pl.ds(lo, cw)],
                preferred_element_type=f32).astype(bf16)
            for core in range(2):
                n = block_rows // 2
                real = field[core * n:(core + 1) * n]
                imag = field[block_rows + core * n:block_rows + (core + 1) * n]
                at = core * side_rows + b * n
                e_ref[at:at + n, 0:cw] = real
                e_ref[rows + at:rows + at + n, 0:cw] = imag
                e_ref[at:at + n, cw:2 * cw] = -imag
                e_ref[rows + at:rows + at + n, cw:2 * cw] = real

    def product(lo, cw, v, k):
        at = v * vw
        if cw < BIG:
            both = jnp.concatenate(
                [g_ref[k, pl.ds(lo, cw), at:at + vw],
                 g_ref[k, pl.ds(lo, cw), pixels + at:pixels + at + vw]], axis=0)
            return jnp.dot(e_ref[:, 0:2 * cw], both, preferred_element_type=f32)
        amp = jnp.dot(e_ref[:, 0:cw], g_ref[k, pl.ds(lo, cw), at:at + vw],
                      preferred_element_type=f32)
        return amp + jnp.dot(e_ref[:, cw:2 * cw],
                             g_ref[k, pl.ds(lo, cw), pixels + at:pixels + at + vw],
                             preferred_element_type=f32)

    def images(lo, cw):
        def image(kb, inner):
            for i in range(unroll):
                for v in range(part_v):
                    acc_ref[kb * unroll + i, v] += product(lo, cw, v, kb * unroll + i)
            return inner

        lax.fori_loop(0, kers // unroll, image, 0)

    def step(c, carry):
        for cc in range(bigs):
            @pl.when(c == cc)
            def _():
                halos[cc].wait_recv()

        @pl.when(c < bigs)
        def _():
            conv(c, pl.multiple_of(c * BIG, BIG), BIG)

        @pl.when(c == bigs)
        def _():
            def small(s, inner):
                for ss in range(SMALLS):
                    @pl.when(s == ss)
                    def _():
                        halos[bigs + ss].wait_recv()
                conv(bigs + s, pl.multiple_of(bigs * BIG + s * SMALL, SMALL), SMALL)
                return inner

            lax.fori_loop(0, SMALLS, small, 0)

        @pl.when(c == 1)
        def _():
            for copy in g_copies:
                copy.wait()

        @pl.when(c > 0)
        def _():
            lo = pl.multiple_of((c - 1) * BIG, BIG)
            gather(c - 1, lo, BIG)
            images(lo, BIG)

        return carry

    lax.fori_loop(0, bigs + 1, step, 0)
    for c in range(bigs, chunks - 1):
        gather(c, edges[c], SMALL)
        images(edges[c], SMALL)
    gather(chunks - 1, edges[-2], SMALL)

    weight = source_w[me // groups]
    chip = me // 2
    chips = tiles // 2

    def ret_copy(n, h, i):
        return pltpu.make_async_remote_copy(
            src_ref=r_ref.at[n, i, h], dst_ref=rr_ref.at[n, sec, chip],
            send_sem=ret_send.at[n], recv_sem=ret_recv.at[n],
            device_id=(h, 2 * i + side), device_id_type=MESH)

    cx_copies = []

    def ret_block(n):
        cx_copies[n].wait_recv()
        mine = s_ref[pl.ds(pl.multiple_of(side * side_rows, 16), side_rows), n * pw:(n + 1) * pw]
        mine = mine + cx_ref[n]
        for i in range(chips):
            for h in range(2):
                first = i * units + h * half
                r_ref[n, i, h] = mine[first:first + half].astype(bf16)

        def ret_go(i, carry):
            peer = lax.rem(chip + i, chips)
            ret_copy(n, sec, peer).start()
            ret_copy(n, 1 - sec, peer).start()
            return carry

        lax.fori_loop(1, chips, ret_go, 0)
        ret_copy(n, 1 - sec, chip).start()
        pltpu.make_async_copy(r_ref.at[n, chip, sec], rr_ref.at[n, sec, chip], ret_recv.at[n]).start()

    for n in range(SENDS):
        for m in range(per_send):
            v = n * per_send + m

            def power(kb, total):
                for i in range(unroll):
                    k = kb * unroll + i
                    amp = acc_ref[k, v] + product(edges[-2], SMALL, v, k)
                    square = amp * amp
                    total = total + (square[0:rows] + square[rows:])
                return total

            total = jnp.zeros((rows, vw), f32)
            if kers == unroll:
                total = power(0, total)
            else:
                total = lax.fori_loop(0, kers // unroll, power, total)
            s_ref[:, v * vw:(v + 1) * vw] = total * weight
        copy = pltpu.make_async_remote_copy(
            src_ref=s_ref.at[pl.ds(pl.multiple_of((1 - side) * side_rows, 16), side_rows),
                             pl.ds(n * pw, pw)],
            dst_ref=cx_ref.at[n], send_sem=cx_send.at[n], recv_sem=cx_recv.at[n],
            device_id=(sec, sibling), device_id_type=MESH)
        copy.start()
        cx_copies.append(copy)
        if n:
            ret_block(n - 1)
    ret_block(SENDS - 1)

    for n in range(SENDS):
        pltpu.make_async_copy(rr_ref.at[n], rr_ref.at[n], ret_recv.at[n]).wait()

    sent = feat.at[:, sec]
    pltpu.make_async_copy(sent, sent, halo_send).wait()
    for c in range(chunks):
        sent = nr_ref.at[pl.ds(0, (tiles - 1) * SLOT), pl.ds(edges[c], edges[c + 1] - edges[c])]
        pltpu.make_async_copy(sent, sent, near_send.at[c]).wait()
    for n in range(SENDS):
        cx_copies[n].wait_send()

        def ret_sent(i, carry):
            ret_copy(n, sec, 0).wait_send()
            ret_copy(n, 1 - sec, 0).wait_send()
            return carry

        lax.fori_loop(1, chips, ret_sent, 0)
        ret_copy(n, 1 - sec, 0).wait_send()


def on_device(features, conv_weight, head_weight, kernels, source_weights):
    tiles = lax.axis_size("tile")
    groups = tiles // ANG
    _, rows_dev, pixels, chans = features.shape
    half = rows_dev // 2
    units = 2 * half
    kers = kernels.shape[0]
    rows = tiles * units
    bt = min(tiles, 16)
    chunks = (pixels - SMALLS * SMALL) // BIG + SMALLS
    bf16, f32 = jnp.bfloat16, jnp.float32
    feat = features.reshape(half, 2, pixels, chans)
    any_spec = pl.BlockSpec(memory_space=pl.ANY)
    arrived = pl.pallas_call(
        functools.partial(kernel, tiles, groups),
        out_shape=jax.ShapeDtypeStruct((SENDS, 2, tiles // 2, half, pixels // SENDS), bf16),
        in_specs=[
            any_spec,
            any_spec,
            pl.BlockSpec(memory_space=pltpu.VMEM),
            any_spec,
            pl.BlockSpec(memory_space=pltpu.SMEM),
        ],
        out_specs=pl.BlockSpec(memory_space=pl.ANY),
        scratch_shapes=[
            pltpu.VMEM((units, pixels + 2 * PAD, chans), bf16),
            pltpu.VMEM((3, TAPS, 2 * chans, 2 * chans), bf16),
            pltpu.VMEM((BIG, (units // 2 - 1) * TAPS * 2 * chans), bf16),
            pltpu.VMEM((2, pixels, 2 * chans), f32),
            pltpu.VMEM((BIG, units * chans), bf16),
            pltpu.VMEM((units * chans, ANG * SLOT), bf16),
            pltpu.VMEM((2 * bt * units, bt * SLOT), bf16),
            pltpu.VMEM((ANG * SLOT, pixels), bf16),
            pltpu.VMEM((tiles * SLOT, pixels), bf16),
            pltpu.VMEM((2 * rows, 2 * BIG), bf16),
            pltpu.VMEM((kers, pixels // 256, 2 * rows, 256), f32),
            pltpu.VMEM((kers, pixels, 2 * pixels), bf16),
            pltpu.VMEM((rows, pixels), f32),
            pltpu.VMEM((SENDS, rows // 2, pixels // SENDS), f32),
            pltpu.VMEM((SENDS, tiles // 2, 2, half, pixels // SENDS), bf16),
            pltpu.SemaphoreType.DMA,
            pltpu.SemaphoreType.DMA((10,)),
            pltpu.SemaphoreType.DMA((kers,)),
            pltpu.SemaphoreType.DMA,
            pltpu.SemaphoreType.DMA((chunks,)),
            pltpu.SemaphoreType.DMA((chunks,)),
            pltpu.SemaphoreType.DMA((chunks,)),
            pltpu.SemaphoreType.DMA((SENDS,)),
            pltpu.SemaphoreType.DMA((SENDS,)),
            pltpu.SemaphoreType.DMA((SENDS,)),
            pltpu.SemaphoreType.DMA((SENDS,)),
            pltpu.SemaphoreType.REGULAR,
            pltpu.SemaphoreType.REGULAR,
        ],
        compiler_params=pltpu.CompilerParams(
            collective_id=0, has_side_effects=True, vmem_limit_bytes=66_000_000),
    )(feat, conv_weight, head_weight.T, kernels, source_weights)
    image = jnp.sum(arrived.astype(f32), axis=2)
    return image.transpose(2, 1, 0, 3).reshape(1, rows_dev, pixels)


def solution(mesh):
    in_specs = (P("tile", "section", None, None), P(), P(), P("tile", None, None), P())
    out_specs = P("tile", "section", None)
    return jax.shard_map(
        on_device, mesh=mesh, in_specs=in_specs, out_specs=out_specs, check_vma=False
    )
```
